32 devices in a mesh: expert: 8 (over z, y), wshard: 4 (over x, core).
Axes of the slice: x: 2, y: 2, z: 4, core: 2. Of those that a mesh axis runs over, the one named last changes fastest.
Arguments:
- hidden: bfloat16 [4096, 2048], P(('expert', 'wshard')), may hold values from -6 to 6
- segment_ids: int32 [32, 128], P(('expert', 'wshard')), may hold values from 0 to 3, never falling along the last dimension, each value on 1 to 64 neighbouring positions
- routes: int32 [4096, 6], P(('expert', 'wshard')), may hold values from 0 to 31, all different within a row; in each aligned block of 128 rows (0 to 127, 128 to 255, ...) at most 32 rows name the same one
- attn_gain: bfloat16 [2048], P('wshard'), may hold values from 0.5 to 1.5
- w_query: bfloat16 [2048, 3072], P('wshard'), may hold values from -0.125 to 0.125
- w_kv_down: bfloat16 [2048, 576], P('wshard'), may hold values from -0.125 to 0.125
- kv_gain: bfloat16 [512], P('wshard'), may hold values from 0.5 to 1.5
- w_kv_up: bfloat16 [512, 4096], P('wshard'), may hold values from -0.25 to 0.25
- w_out: bfloat16 [2048, 2048], P('wshard'), may hold values from -0.375 to 0.375
- ffn_gain: bfloat16 [2048], P('wshard'), may hold values from 0.5 to 1.5
- w_router: bfloat16 [2048, 32], P('wshard'), may hold values from -0.125 to 0.125
- shared_gate: bfloat16 [2048, 2816], P('wshard', 'expert'), may hold values from -0.125 to 0.125
- shared_up: bfloat16 [2048, 2816], P('wshard', 'expert'), may hold values from -0.125 to 0.125
- shared_down: bfloat16 [2048, 2816], P('wshard', 'expert'), may hold values from -0.109375 to 0.109375
- expert_gate: bfloat16 [32, 2048, 1408], P('expert', None, 'wshard'), may hold values from -0.125 to 0.125
- expert_up: bfloat16 [32, 2048, 1408], P('expert', None, 'wshard'), may hold values from -0.125 to 0.125
- expert_down: bfloat16 [32, 2048, 1408], P('expert', None, 'wshard'), may hold values from -0.15625 to 0.15625
- cotangent: bfloat16 [4096, 2048], P(('expert', 'wshard')), may hold values from -6 to 6
Outputs:
- output: bfloat16 [4096, 2048], P(('expert', 'wshard'))
- input_grad: bfloat16 [4096, 2048], P(('expert', 'wshard'))
- attn_gain_grad: float32 [2048], P('wshard')
- w_query_grad: float32 [2048, 3072], P('wshard')
- w_kv_down_grad: float32 [2048, 576], P('wshard')
- kv_gain_grad: float32 [512], P('wshard')
- w_kv_up_grad: float32 [512, 4096], P('wshard')
- w_out_grad: float32 [2048, 2048], P('wshard')
- ffn_gain_grad: float32 [2048], P('wshard')
- w_router_grad: float32 [2048, 32], P('wshard')
- shared_gate_grad: float32 [2048, 2816], P('wshard', 'expert')
- shared_up_grad: float32 [2048, 2816], P('wshard', 'expert')
- shared_down_grad: float32 [2048, 2816], P('wshard', 'expert')
- expert_gate_grad: float32 [32, 2048, 1408], P('expert', None, 'wshard')
- expert_up_grad: float32 [32, 2048, 1408], P('expert', None, 'wshard')
- expert_down_grad: float32 [32, 2048, 1408], P('expert', None, 'wshard')
The draws below stay inside these ranges and needn't reach their ends.
Inputs may be any that keep to these rules, and one draw needn't show every extreme that they name: `segment_ids`: along each row (one device's tokens) the ids never fall; each sequence has 1 to 64 tokens, and one has exactly 64. `routes`: each token names 6 different experts. Among the 128 tokens of one device, no expert is named by more than 32 tokens, and in every draw some expert is named by exactly 32 tokens of some device. Every expert is named somewhere.
All inputs are finite; a program needn't handle non-finite values.
Results may differ from the reference program's by a relative error of at most 0.024.
Values may be sent and summed in bfloat16 or wider, within the bound.
No kernel may reach another device: no remote copies, remote signals or barrier semaphores. Data moves between devices by JAX's collectives and lax.ppermute only.
A program may use at most 512 MiB of HBM per device.

```python
import math
import jax
import jax.numpy as jnp
import numpy as np
from jax import lax

D = 2048
HEADS = 16
NOPE = 128
ROPE = 64
VH = 128
KVR = 512
FF = 1408
TOP = 6
FS = 2816
EXPERTS = 32
SEGS = 4
TOK_DEV = 128
MAXLEN = 64
CAP = 32
TOKENS = 4096
N_EXPERT = 8
N_WSHARD = 4


def levels(own_key, shape, split, smallest, high):
    level = 1.0
    for dim, blocks in split:
        heights = jax.random.uniform(jax.random.fold_in(jax.random.fold_in(own_key, 6), dim), (blocks,), jnp.float32, smallest / len(split), high / len(split))
        level = level * jnp.repeat(jnp.exp(heights), shape[dim] // blocks).reshape((-1,) + (1,) * (len(shape) - 1 - dim))
    return level


def length_profile(amount, total, bound, slope):
    weights = [(1 << 20) // math.isqrt(rank ** slope) + 1 for rank in range(2, amount + 1)]
    spare, given = total - bound - (amount - 1), [1] * (amount - 1)
    while spare > 0:
        movable = [i for i in range(amount - 1) if given[i] < bound]
        pool, remaining = sum([weights[i] for i in movable]), spare
        for i in movable:
            addition = min(bound - given[i], max(1, remaining * weights[i] // pool), spare)
            given[i] = given[i] + addition
            spare = spare - addition
    return np.array([bound] + given)


def uneven_parts(own_key, number_of, total, limit, skew):
    if number_of == 2:
        one = jax.random.randint(own_key, (), max(1, total - limit), min(limit, total - 1) + 1)
        return jnp.stack([one, total - one])
    lengths = jnp.asarray(length_profile(number_of, total, limit, skew), jnp.int32)
    pairs = (number_of - 1) // 2
    donor, sink = lengths[1:1 + 2 * pairs:2], lengths[2:2 + 2 * pairs:2]
    margin = jnp.minimum(donor - 1, limit - sink)
    moved = jax.random.randint(jax.random.fold_in(own_key, 1), (pairs,), 0, 1 << 20) % (margin + 1)
    lengths = lengths.at[1:1 + 2 * pairs:2].set(donor - moved).at[2:2 + 2 * pairs:2].set(sink + moved)
    return lengths[jax.random.permutation(jax.random.fold_in(own_key, 2), number_of)]


def routed_block(own_key, own, number, rows, count, top, bound, skew):
    order = jax.random.permutation(own_key, count)
    heavy_load, ordinary = load_shares(count, rows * top, bound, skew, True), load_shares(count, rows * top, bound, skew, False)
    places = jnp.arange(count)

    def named(tallies, turn):
        used = int((tallies > 0).sum())
        fixed = max(1, used // 4)
        moved = fixed + (places - fixed + turn * (used - fixed)) % max(1, count - fixed)
        return jnp.zeros((count,), jnp.int32).at[order[jnp.where(places < fixed, places, moved)]].set(jnp.asarray(tallies, jnp.int32))

    tallies = jnp.where(number % 4 == 0, named(heavy_load, number // 4), named(ordinary, number - number // 4 - 1))
    mixed = jax.random.permutation(jax.random.fold_in(own, 3), count)
    giver, receiver = mixed[0:count // 2 * 2:2], mixed[1:count // 2 * 2:2]
    room = jnp.minimum(tallies[giver] - 1, bound - tallies[receiver]) // 2
    room = jnp.where((giver == order[0]) | (receiver == order[0]) | (tallies[receiver] == 0), 0, jnp.maximum(room, 0))
    moved = jax.random.randint(jax.random.fold_in(own, 4), (count // 2,), 0, 1 << 20) % (room + 1)
    tallies = tallies.at[giver].add(-moved).at[receiver].add(moved)
    labels = jnp.searchsorted(jnp.cumsum(tallies), jnp.arange(rows * top), side="right").astype(jnp.int32)
    grid = labels.reshape(top, rows).T
    grid = grid[jax.random.permutation(jax.random.fold_in(own, 1), rows)]
    turn = jax.random.randint(jax.random.fold_in(own, 2), (rows, 1), 0, top)
    return jnp.take_along_axis(grid, (jnp.arange(top)[None, :] + turn) % top, axis=1)


def load_shares(number_of, total, limit, slope, full):
    loads = [(1 << 20) // math.isqrt(grade ** slope) + 1 for grade in range(1, number_of + 1)]
    largest = limit if full else min(limit, max(-(-total // number_of), total * loads[0] // sum(loads)))
    least = 1 if total - largest >= number_of - 1 else 0
    holding, spare = [largest] + [least] * (number_of - 1), total - largest - least * (number_of - 1)
    while spare > 0:
        free = [i for i in range(1, number_of) if holding[i] < largest] or [i for i in range(1, number_of) if holding[i] < limit]
        whole, remaining = sum([loads[i] for i in free]), spare
        for i in free:
            addition = min(limit - holding[i], max(1, remaining * loads[i] // whole), spare)
            holding[i] = holding[i] + addition
            spare = spare - addition
    return np.array(holding)


def normal_values(rng, dims, deviation, reach, shards=(), kind=jnp.bfloat16):
    values = deviation * jax.random.normal(rng, dims, jnp.float32)
    if shards:
        values = values * levels(rng, dims, shards, -0.22, 0.18)
    return jnp.clip(values, -reach, reach).astype(kind)


def setup_inputs(seed: int = 0) -> dict:
    key_list = jax.random.split(jax.random.key(seed), 19)
    hidden = normal_values(key_list[0], (TOKENS, D), 1.0, 6.0, ((0, 32),))
    segment_ids = jax.vmap(lambda own: jnp.searchsorted(jnp.cumsum(uneven_parts(own, SEGS, TOK_DEV, MAXLEN, 2)), jnp.arange(TOK_DEV), side="right"))(jax.random.split(key_list[1], (N_EXPERT * N_WSHARD))).reshape((N_EXPERT * N_WSHARD, TOK_DEV)).astype(jnp.int32)
    routes_keys = jax.random.split(jax.random.fold_in(key_list[2], 1), TOKENS // TOK_DEV)
    routes_turns = jax.random.permutation(jax.random.fold_in(key_list[2], 3), TOKENS // TOK_DEV)
    routes = jax.vmap(lambda own, number: routed_block(jax.random.fold_in(key_list[2], 2), own, number, TOK_DEV, EXPERTS, TOP, CAP, 2))(routes_keys, routes_turns).reshape((TOKENS, TOP))
    attn_gain = jnp.clip(1.0 + 0.1 * jax.random.normal(key_list[3], (D,), jnp.float32), 0.5, 1.5).astype(jnp.bfloat16)
    w_query = normal_values(key_list[4], (D, HEADS * (NOPE + ROPE)), D ** -0.5, 0.125, ((0, 4),))
    w_kv_down = normal_values(key_list[5], (D, KVR + ROPE), D ** -0.5, 0.125, ((0, 4),))
    kv_gain = jnp.clip(1.0 + 0.1 * jax.random.normal(key_list[6], (KVR,), jnp.float32), 0.5, 1.5).astype(jnp.bfloat16)
    w_kv_up = normal_values(key_list[7], (KVR, HEADS * (NOPE + VH)), KVR ** -0.5, 0.25, ((0, 4),))
    w_out = normal_values(key_list[8], (HEADS * VH, D), (HEADS * VH // 8) ** -0.5, 0.375, ((0, 4),))
    ffn_gain = jnp.clip(1.0 + 0.1 * jax.random.normal(key_list[9], (D,), jnp.float32), 0.5, 1.5).astype(jnp.bfloat16)
    w_router = normal_values(key_list[10], (D, EXPERTS), D ** -0.5, 0.125, ((0, 4),))
    shared_gate = normal_values(key_list[11], (D, FS), D ** -0.5, 0.125, ((0, 4), (1, 8)))
    shared_up = normal_values(key_list[12], (D, FS), D ** -0.5, 0.125, ((0, 4), (1, 8)))
    shared_down = normal_values(key_list[13], (D, FS), FS ** -0.5, 0.109375, ((0, 4), (1, 8)))
    expert_gate = normal_values(key_list[14], (EXPERTS, D, FF), D ** -0.5, 0.125, ((0, 8), (2, 4)))
    expert_up = normal_values(key_list[15], (EXPERTS, D, FF), D ** -0.5, 0.125, ((0, 8), (2, 4)))
    expert_down = normal_values(key_list[16], (EXPERTS, D, FF), FF ** -0.5, 0.15625, ((0, 8), (2, 4)))
    cotangent = normal_values(key_list[17], (TOKENS, D), 1.0, 6.0, ((0, 32),))
    return dict(hidden=hidden, segment_ids=segment_ids, routes=routes, attn_gain=attn_gain, w_query=w_query, w_kv_down=w_kv_down, kv_gain=kv_gain, w_kv_up=w_kv_up, w_out=w_out, ffn_gain=ffn_gain, w_router=w_router, shared_gate=shared_gate, shared_up=shared_up, shared_down=shared_down, expert_gate=expert_gate, expert_up=expert_up, expert_down=expert_down, cotangent=cotangent)


EPS = 1e-06
THETA = 50000.0

def dot_last(left, right):
    return jnp.dot(left, right, preferred_element_type=jnp.float32)

def dot_rows(left, right):
    return lax.dot_general(left, right, (((0,), (0,)), ((), ())), preferred_element_type=jnp.float32)

def dot_cols(left, right):
    return lax.dot_general(left, right, (((1,), (1,)), ((), ())), preferred_element_type=jnp.float32)

def batched(form, left, right):
    return jnp.einsum(form, left.astype(jnp.float32), right.astype(jnp.float32))

def round_trip(vector):
    return lax.optimization_barrier(vector.astype(jnp.bfloat16)).astype(jnp.float32)

def rms_norm(values, gain):
    inverse = lax.rsqrt(lax.optimization_barrier(jnp.mean(values * values, axis=-1, keepdims=True)) + EPS)
    return (values * inverse * gain, inverse)

def rms_back(values, inverse, gain, grad_in):
    scaled = grad_in * gain
    gain_grad = lax.optimization_barrier(jnp.sum(grad_in * values * inverse, axis=0))
    moment = lax.optimization_barrier(jnp.mean(scaled * values, axis=-1, keepdims=True))
    return (inverse * scaled - values * inverse ** 3 * moment, gain_grad)

def segment_positions(segment):
    places = jnp.arange(segment.shape[0], dtype=jnp.int32)
    earlier = lax.optimization_barrier(jnp.sum((segment[None, :] < segment[:, None]).astype(jnp.int32), axis=1)).astype(jnp.int32)
    return (places - earlier).astype(jnp.float32)

def rope_tables(segment):
    position = segment_positions(segment)
    inverse_freq = THETA ** (-jnp.arange(ROPE // 2, dtype=jnp.float32) * 2.0 / ROPE)
    angles = position[:, None] * inverse_freq[None, :]
    cosine = jnp.concatenate([jnp.cos(angles), jnp.cos(angles)], axis=1)
    sine_tab = jnp.concatenate([jnp.sin(angles), jnp.sin(angles)], axis=1)
    return (cosine, sine_tab)

def rotate_half(vector):
    half_size = vector.shape[-1] // 2
    return jnp.concatenate([-vector[..., half_size:], vector[..., :half_size]], axis=-1)

def apply_rope(vector, cosine, sine_tab):
    return vector * cosine + rotate_half(vector) * sine_tab

def rope_back(grad_in, cosine, sine_tab):
    return grad_in * cosine - rotate_half(grad_in * sine_tab)

def allowed_mask(segment):
    places = jnp.arange(segment.shape[0], dtype=jnp.int32)
    return (segment[:, None] == segment[None, :]) & (places[None, :] <= places[:, None])

def attend_forward(tokens, segment, attn_gain, w_query, w_kv_down, kv_gain, w_kv_up, w_out):
    tok_count = tokens.shape[0]
    cosine, sine_tab = rope_tables(segment)
    scale_qk = 1.0 / math.sqrt(NOPE + ROPE)
    inputs = tokens.astype(jnp.float32)
    normed_f, inverse_one = rms_norm(inputs, attn_gain.astype(jnp.float32))
    normed_b = normed_f.astype(jnp.bfloat16)
    query_f = dot_last(normed_b, w_query).reshape(tok_count, HEADS, NOPE + ROPE)
    query_rot = apply_rope(query_f[..., NOPE:], cosine[:, None, :], sine_tab[:, None, :])
    queries = jnp.concatenate([query_f[..., :NOPE], query_rot], axis=2).astype(jnp.bfloat16)
    lowered = dot_last(normed_b, w_kv_down)
    latent = lowered[:, :KVR]
    latent_f, inverse_kv = rms_norm(latent, kv_gain.astype(jnp.float32))
    latent_b = latent_f.astype(jnp.bfloat16)
    key_rope = apply_rope(lowered[:, KVR:], cosine, sine_tab)
    raised_kv = dot_last(latent_b, w_kv_up).reshape(tok_count, HEADS, NOPE + VH)
    shared_rope = jnp.broadcast_to(key_rope[:, None, :], (tok_count, HEADS, ROPE))
    key_vals = jnp.concatenate([raised_kv[..., :NOPE], shared_rope], axis=2).astype(jnp.bfloat16)
    values = raised_kv[..., NOPE:].astype(jnp.bfloat16)
    allowed = allowed_mask(segment)
    scores = batched('ihd,jhd->hij', queries, key_vals) * scale_qk
    raised = jnp.where(allowed[None], jnp.exp(scores), 0.0)
    totals = lax.optimization_barrier(jnp.sum(raised, axis=2))
    attn_probs = (raised / totals[:, :, None]).astype(jnp.bfloat16)
    context = batched('hij,jhd->ihd', attn_probs, values).astype(jnp.bfloat16).reshape(tok_count, HEADS * VH)
    mixed_out = inputs + dot_last(context, w_out)
    kept_state = (normed_b, inverse_one, inputs, latent, inverse_kv, latent_b, queries, key_vals, values, jnp.log(totals), context)
    return (mixed_out, kept_state)

def attend_backward(grad_in, segment, attn_gain, w_query, w_kv_down, kv_gain, w_kv_up, w_out, kept_state):
    normed_b, inverse_one, inputs, latent, inverse_kv, latent_b, queries, key_vals, values, log_totals, context = kept_state
    tok_count = grad_in.shape[0]
    cosine, sine_tab = rope_tables(segment)
    scale_qk = 1.0 / math.sqrt(NOPE + ROPE)
    grad_b = grad_in.astype(jnp.bfloat16)
    out_w_grad = dot_rows(context, grad_b)
    context_grad = dot_cols(grad_b, w_out).astype(jnp.bfloat16).reshape(tok_count, HEADS, VH)
    allowed = allowed_mask(segment)
    scores = batched('ihd,jhd->hij', queries, key_vals) * scale_qk
    attn_back = jnp.where(allowed[None], jnp.exp(scores - log_totals[:, :, None]), 0.0)
    value_grad = batched('hij,ihd->jhd', attn_back.astype(jnp.bfloat16), context_grad)
    prob_grad = batched('ihd,jhd->hij', context_grad, values)
    context_h = context.reshape(tok_count, HEADS, VH).astype(jnp.float32)
    delta_sum = lax.optimization_barrier(jnp.sum(context_grad.astype(jnp.float32) * context_h, axis=2)).T
    score_grad = (attn_back * (prob_grad - delta_sum[:, :, None]) * scale_qk).astype(jnp.bfloat16)
    query_grad = batched('hij,jhd->ihd', score_grad, key_vals)
    key_grad = batched('hij,ihd->jhd', score_grad, queries)
    query_rot = rope_back(query_grad[..., NOPE:], cosine[:, None, :], sine_tab[:, None, :])
    query_flat = jnp.concatenate([query_grad[..., :NOPE], query_rot], axis=2).astype(jnp.bfloat16).reshape(tok_count, -1)
    key_rope = rope_back(lax.optimization_barrier(jnp.sum(key_grad[..., NOPE:], axis=1)), cosine, sine_tab)
    up_grad = jnp.concatenate([key_grad[..., :NOPE], value_grad], axis=2).astype(jnp.bfloat16).reshape(tok_count, -1)
    kv_up_grad = dot_rows(latent_b, up_grad)
    latent_up = dot_cols(up_grad, w_kv_up)
    latent_grad, kv_gain_grad = rms_back(latent, inverse_kv, kv_gain.astype(jnp.float32), latent_up)
    down_grad = jnp.concatenate([latent_grad, key_rope], axis=1).astype(jnp.bfloat16)
    kv_down_grad = dot_rows(normed_b, down_grad)
    query_w_grad = dot_rows(normed_b, query_flat)
    normed_grad = dot_cols(query_flat, w_query) + dot_cols(down_grad, w_kv_down)
    hidden_part, attn_gain_grad = rms_back(inputs, inverse_one, attn_gain.astype(jnp.float32), normed_grad)
    return (grad_in + hidden_part, (attn_gain_grad, query_w_grad, kv_down_grad, kv_gain_grad, kv_up_grad, out_w_grad))

def route_weights(normed, router_w, routes):
    logits = dot_last(normed, router_w)
    choose = (routes[:, :, None] == jnp.arange(EXPERTS, dtype=jnp.int32)[None, None, :]).astype(jnp.float32)
    chosen = lax.optimization_barrier(jnp.sum(choose * logits[:, None, :], axis=2))
    exp_chosen = jnp.exp(chosen)
    return (choose, exp_chosen / lax.optimization_barrier(jnp.sum(exp_chosen, axis=1, keepdims=True)))

def slot_table(routes):
    tok_count = routes.shape[0]
    flat_ids = routes.reshape(-1)
    onehot = (flat_ids[:, None] == jnp.arange(EXPERTS, dtype=jnp.int32)[None, :]).astype(jnp.int32)
    before = jnp.cumsum(onehot, axis=0) - onehot
    rank_in = lax.optimization_barrier(jnp.sum(before * onehot, axis=1))
    slot_of = (flat_ids * CAP + rank_in).astype(jnp.int32)
    matches = slot_of[None, :] == jnp.arange(EXPERTS * CAP, dtype=jnp.int32)[:, None]
    owners = jnp.arange(tok_count * TOP, dtype=jnp.int32) // TOP
    slot_token = lax.optimization_barrier(jnp.sum(jnp.where(matches, owners[None, :], 0), axis=1)).astype(jnp.int32)
    is_live = jnp.any(matches, axis=1)
    return (slot_of, matches, slot_token, is_live)

def expert_forward(row_block, gate_w, up_w, down_w):
    gate_act = batched('jmd,jdf->jmf', row_block, gate_w)
    upper_act = batched('jmd,jdf->jmf', row_block, up_w)
    active = (gate_act * jax.nn.sigmoid(gate_act) * upper_act).astype(jnp.bfloat16)
    output = batched('jmf,jdf->jmd', active, down_w)
    return (output, gate_act, upper_act, active)

def expert_backward(row_block, out_grad, gate_w, up_w, down_w, gate_act, upper_act, active):
    act_grad = batched('jmd,jdf->jmf', out_grad, down_w)
    down_grad = batched('jmd,jmf->jdf', out_grad, active)
    sigmoid_v = jax.nn.sigmoid(gate_act)
    up_part = (act_grad * gate_act * sigmoid_v).astype(jnp.bfloat16)
    gate_part = (act_grad * upper_act * sigmoid_v * (1.0 + gate_act * (1.0 - sigmoid_v))).astype(jnp.bfloat16)
    gate_grad = batched('jmd,jmf->jdf', row_block, gate_part)
    up_grad = batched('jmd,jmf->jdf', row_block, up_part)
    row_grad = batched('jmf,jdf->jmd', gate_part, gate_w) + batched('jmf,jdf->jmd', up_part, up_w)
    return (row_grad, gate_grad, up_grad, down_grad)

def reference(hidden, segment_ids, routes, attn_gain, w_query, w_kv_down, kv_gain, w_kv_up, w_out, ffn_gain, w_router, shared_gate, shared_up, shared_down, expert_gate, expert_up, expert_down, cotangent):
    devices = segment_ids.shape[0]
    blocks = hidden.reshape(devices, TOK_DEV, D)
    attn_weights = (attn_gain, w_query, w_kv_down, kv_gain, w_kv_up, w_out)

    def forward_block(block_pair):
        mixed_out, kept_state = attend_forward(block_pair[0], block_pair[1], attn_gain, w_query, w_kv_down, kv_gain, w_kv_up, w_out)
        return mixed_out
    middle = lax.map(forward_block, (blocks, segment_ids)).reshape(-1, D)
    normed_f, inverse_two = rms_norm(middle, ffn_gain.astype(jnp.float32))
    normed = normed_f.astype(jnp.bfloat16)
    choose, weights = route_weights(normed, w_router, routes)
    shared_res = expert_forward(normed[None], shared_gate[None], shared_up[None], shared_down[None])
    shared_out = shared_res[0][0]

    def table_block(block_pair):
        slot_of, matches, slot_token, is_live = slot_table(block_pair[0])
        slot_weight = lax.optimization_barrier(jnp.sum(jnp.where(matches, block_pair[1].reshape(-1)[None, :], 0.0), axis=1))
        return (slot_of, slot_token, is_live, slot_weight)
    slot_of, slot_token, is_live, slot_weight = lax.map(table_block, (routes.reshape(devices, TOK_DEV, TOP), weights.reshape(devices, TOK_DEV, TOP)))
    offsets = (jnp.arange(devices, dtype=jnp.int32) * TOK_DEV)[:, None]
    cot_f = cotangent.astype(jnp.float32)

    def expert_step(carried, expert_id):
        routed, row_back = carried
        token_index = (lax.dynamic_slice_in_dim(slot_token, expert_id * CAP, CAP, axis=1) + offsets).reshape(-1)
        alive_mask = lax.dynamic_slice_in_dim(is_live, expert_id * CAP, CAP, axis=1).reshape(-1)
        share_w = lax.dynamic_slice_in_dim(slot_weight, expert_id * CAP, CAP, axis=1).reshape(-1)
        row_block = jnp.where(alive_mask[:, None], jnp.take(normed, token_index, axis=0), jnp.zeros((), jnp.bfloat16))
        upstream = jnp.take(cot_f, token_index, axis=0)
        out_grad = (share_w[:, None] * upstream).astype(jnp.bfloat16)
        gate_w = lax.dynamic_slice_in_dim(expert_gate, expert_id, 1, axis=0)
        up_w = lax.dynamic_slice_in_dim(expert_up, expert_id, 1, axis=0)
        down_w = lax.dynamic_slice_in_dim(expert_down, expert_id, 1, axis=0)
        output, gate_act, upper_act, active = expert_forward(row_block[None], gate_w, up_w, down_w)
        out_rows = round_trip(output[0])
        row_grad, gate_grad, up_grad, down_grad = expert_backward(row_block[None], out_grad[None], gate_w, up_w, down_w, gate_act, upper_act, active)
        routed = routed.at[token_index].add(share_w[:, None] * out_rows)
        row_back = row_back.at[token_index].add(round_trip(row_grad[0]))
        slot_dots = lax.optimization_barrier(jnp.sum(upstream * out_rows, axis=1))
        return ((routed, row_back), (gate_grad[0], up_grad[0], down_grad[0], slot_dots))
    zero_rows = jnp.zeros((devices * TOK_DEV, D), jnp.float32)
    (routed, row_back), (gate_grads, up_grads, down_grads, slot_dots) = lax.scan(expert_step, (zero_rows, zero_rows), jnp.arange(EXPERTS, dtype=jnp.int32))
    dot_map = slot_dots.reshape(EXPERTS, devices, CAP).transpose(1, 0, 2).reshape(devices, EXPERTS * CAP)
    weight_dots = jnp.take_along_axis(dot_map, slot_of, axis=1).reshape(-1, TOP)
    output = (middle + shared_out + routed).astype(jnp.bfloat16)
    mixed_w = weights * (weight_dots - lax.optimization_barrier(jnp.sum(weights * weight_dots, axis=1, keepdims=True)))
    logit_grad = lax.optimization_barrier(jnp.sum(mixed_w[:, :, None] * choose, axis=1)).astype(jnp.bfloat16)
    router_grad = dot_rows(normed, logit_grad)
    shared_back = expert_backward(normed[None], cotangent[None], shared_gate[None], shared_up[None], shared_down[None], shared_res[1], shared_res[2], shared_res[3])
    normed_grad = dot_cols(logit_grad, w_router) + shared_back[0][0] + row_back
    middle_part, ffn_gain_grad = rms_back(middle, inverse_two, ffn_gain.astype(jnp.float32), normed_grad)
    middle_grad = cot_f + middle_part

    def backward_block(carried, block_items):
        tokens, segment, grad_in = block_items
        mixed_out, kept_state = attend_forward(tokens, segment, attn_gain, w_query, w_kv_down, kv_gain, w_kv_up, w_out)
        input_part, grad_list = attend_backward(grad_in, segment, attn_gain, w_query, w_kv_down, kv_gain, w_kv_up, w_out, kept_state)
        return (jax.tree.map(jnp.add, carried, grad_list), input_part.astype(jnp.bfloat16))
    start_grads = tuple((jnp.zeros(weight.shape, jnp.float32) for weight in attn_weights))
    grad_sums, input_grad = lax.scan(backward_block, start_grads, (blocks, segment_ids, middle_grad.reshape(devices, TOK_DEV, D)))
    return (output, input_grad.reshape(-1, D), grad_sums[0], grad_sums[1], grad_sums[2], grad_sums[3], grad_sums[4], grad_sums[5], ffn_gain_grad, router_grad, shared_back[1][0], shared_back[2][0], shared_back[3][0], gate_grads, up_grads, down_grads)
```

```python
import math

import jax
import jax.numpy as jnp
from jax import lax
from jax.sharding import PartitionSpec as P

NOPE = 128
ROPE = 64
VH = 128
CAP = 32
EPS = 1e-06
THETA = 50000.0

EX = "expert"
WS = "wshard"
ALL = (EX, WS)

BF = jnp.bfloat16
F32 = jnp.float32


def ein(form, left, right):
    return jnp.einsum(form, left, right, preferred_element_type=F32)


def ein_b(form, left, right):
    return jnp.einsum(form, left, right, preferred_element_type=BF)


def rms_norm(values, gain):
    inverse = lax.rsqrt(jnp.mean(values * values, axis=-1, keepdims=True) + EPS)
    return (values * inverse * gain, inverse)


def rms_back(values, inverse, gain, grad_in):
    scaled = grad_in * gain
    gain_grad = jnp.sum(grad_in * values * inverse, axis=0)
    moment = jnp.mean(scaled * values, axis=-1, keepdims=True)
    return (inverse * scaled - values * inverse**3 * moment, gain_grad)


def rope_tables(segment):
    places = jnp.arange(segment.shape[1], dtype=jnp.int32)
    earlier = jnp.sum((segment[:, None, :] < segment[:, :, None]).astype(jnp.int32), axis=2)
    position = (places[None, :] - earlier).astype(F32)
    inverse_freq = THETA ** (-jnp.arange(ROPE // 2, dtype=F32) * 2.0 / ROPE)
    angles = position[:, :, None] * inverse_freq[None, None, :]
    cosine = jnp.cos(angles)
    sine = jnp.sin(angles)
    return (
        jnp.concatenate([cosine, cosine], axis=2),
        jnp.concatenate([sine, sine], axis=2),
    )


def rotate_half(vector):
    half_size = vector.shape[-1] // 2
    return jnp.concatenate([-vector[..., half_size:], vector[..., :half_size]], axis=-1)


def apply_rope(vector, cosine, sine):
    return vector * cosine + rotate_half(vector) * sine


def rope_back(grad_in, cosine, sine):
    return grad_in * cosine - rotate_half(grad_in * sine)


def bits_of(size):
    bit = size // 2
    bits = []
    while bit:
        bits.append(bit)
        bit //= 2
    return bits


def swap(x, axis, bit):
    size = lax.axis_size(axis)
    return lax.ppermute(x, axis, [(i, i ^ bit) for i in range(size)])


def rel_ids(size):
    ids = [0]
    for bit in bits_of(size):
        ids = ids + [i ^ bit for i in ids]
    return ids


def gather_rel(x, axis):
    buf = x[None]
    for bit in bits_of(lax.axis_size(axis)):
        buf = jnp.concatenate([buf, swap(buf, axis, bit)], axis=0)
    return buf


def scatter_rel(x, axis):
    buf = x.astype(F32)
    for bit in reversed(bits_of(lax.axis_size(axis))):
        half = buf.shape[0] // 2
        other = swap(buf[half:].astype(BF), axis, bit)
        buf = buf[:half] + other.astype(F32)
    return buf[0]


def local(
    hidden,
    segment_ids,
    routes,
    attn_gain,
    w_query,
    w_kv_down,
    kv_gain,
    w_kv_up,
    w_out,
    ffn_gain,
    w_router,
    shared_gate,
    shared_up,
    shared_down,
    expert_gate,
    expert_up,
    expert_down,
    cotangent,
):
    n_ex = lax.axis_size(EX)
    n_ws = lax.axis_size(WS)
    n_dev = n_ex * n_ws
    e_rank = lax.axis_index(EX)
    w_rank = lax.axis_index(WS)
    d_rank = e_rank * n_ws + w_rank
    tok, width = hidden.shape
    top = routes.shape[1]
    d_part = w_query.shape[0]
    kv_part = w_kv_up.shape[0]
    kvr = kv_part * n_ws
    heads = w_out.shape[0] // VH
    hq = NOPE + ROPE
    n_local = expert_gate.shape[0]
    experts = n_local * n_ex
    fs_part = shared_gate.shape[1] // n_ws
    lanes = 128
    chunks = max(1, n_dev // 32)

    small = jnp.concatenate(
        [
            w_router.T.reshape(-1, lanes),
            attn_gain.reshape(-1, lanes),
            ffn_gain.reshape(-1, lanes),
            kv_gain.reshape(-1, lanes),
            segment_ids.astype(BF).reshape(-1, lanes),
        ],
        axis=0,
    )
    small = lax.all_gather(small, WS, axis=0, tiled=False)
    r0 = experts * d_part // lanes
    r1 = r0 + d_part // lanes
    r2 = r1 + d_part // lanes
    r3 = r2 + kv_part // lanes
    router_t = (
        small[:, :r0].reshape(n_ws, experts, d_part).transpose(1, 0, 2).reshape(experts, width)
    )
    gain_one = small[:, r0:r1].reshape(width).astype(F32)
    gain_two = small[:, r1:r2].reshape(width).astype(F32)
    gain_kv = small[:, r2:r3].reshape(kvr).astype(F32)
    segment_abs = small[:, r3:].reshape(n_ws, tok).astype(jnp.int32)
    ids = jnp.array(rel_ids(n_ws), dtype=jnp.int32)
    segment = jnp.take(segment_abs, w_rank ^ ids, axis=0)

    hidden_g = gather_rel(hidden, WS)
    wq = lax.all_to_all(w_query, WS, split_axis=1, concat_axis=0, tiled=True)
    wkv = lax.all_to_all(w_kv_up, WS, split_axis=1, concat_axis=0, tiled=True)
    wdn = lax.all_gather(w_kv_down, WS, axis=0, tiled=True)

    grp = n_ws * tok
    cosine, sine = rope_tables(segment)
    scale_qk = 1.0 / math.sqrt(hq)
    inputs_g = hidden_g.reshape(grp, width).astype(F32)
    normed_f, inverse_g = rms_norm(inputs_g, gain_one)
    normed_in = normed_f.astype(BF)
    query_f = ein("md,df->mf", normed_in, wq).reshape(n_ws, tok, heads, hq)
    query_rot = apply_rope(query_f[..., NOPE:], cosine[:, :, None, :], sine[:, :, None, :])
    queries = jnp.concatenate([query_f[..., :NOPE], query_rot], axis=3).astype(BF)
    lowered = ein("md,df->mf", normed_in, wdn)
    latent = lowered[:, :kvr]
    latent_f, inverse_kv = rms_norm(latent, gain_kv)
    latent_b = latent_f.astype(BF)
    key_rope = apply_rope(lowered[:, kvr:].reshape(n_ws, tok, ROPE), cosine, sine)
    raised_kv = ein("md,df->mf", latent_b, wkv).reshape(n_ws, tok, heads, NOPE + VH)
    key_vals = jnp.concatenate(
        [
            raised_kv[..., :NOPE],
            jnp.broadcast_to(key_rope[:, :, None, :], (n_ws, tok, heads, ROPE)),
        ],
        axis=3,
    ).astype(BF)
    values = raised_kv[..., NOPE:].astype(BF)
    places = jnp.arange(tok, dtype=jnp.int32)
    allowed = (segment[:, :, None] == segment[:, None, :]) & (
        places[None, None, :] <= places[None, :, None]
    )
    scores = ein("bihd,bjhd->bhij", queries, key_vals) * scale_qk
    raised = jnp.where(allowed[:, None], jnp.exp(scores), 0.0)
    totals = jnp.sum(raised, axis=3)
    attn_probs = (raised / totals[..., None]).astype(BF)
    context = ein("bhij,bjhd->bihd", attn_probs, values).astype(BF)
    context_flat = context.reshape(grp, heads * VH)
    mixed = scatter_rel(ein("mf,fd->md", context_flat, w_out).reshape(n_ws, tok, width), WS)
    inputs = hidden.astype(F32)
    middle = inputs + mixed
    normed_two, inverse_two = rms_norm(middle, gain_two)
    normed = normed_two.astype(BF)

    cot_all = lax.all_gather(cotangent, ALL, axis=0, tiled=True)
    routes_all = lax.all_gather(routes.T, ALL, axis=0, tiled=False)
    normed_all = lax.all_gather(normed, ALL, axis=0, tiled=True)

    shared = jnp.stack([shared_gate.T, shared_up.T, shared_down.T], axis=0)
    shared = shared.reshape(3, n_ws, fs_part, d_part).transpose(1, 0, 2, 3)
    shared = lax.all_to_all(shared, WS, split_axis=0, concat_axis=0, tiled=True)
    shared = shared.transpose(1, 2, 0, 3).reshape(3, fs_part, width)
    sgate, sup, sdown = shared[0], shared[1], shared[2]

    tri = (places[:, None] < places[None, :]).astype(BF)

    def picks(table, wanted):
        hit = jnp.any(table[:, None] == wanted[None, :, None, None], axis=2)
        rank = ein("bxs,st->bxt", hit.astype(BF), tri).astype(jnp.int32)
        slot = jnp.arange(CAP, dtype=jnp.int32)
        return hit, (hit[:, :, None, :] & (rank[:, :, None, :] == slot[None, None, :, None]))

    own_experts = e_rank * n_local + jnp.arange(n_local, dtype=jnp.int32)
    _, pick = picks(routes_all, own_experts)
    pick_b = pick.astype(BF)
    every = jnp.arange(experts, dtype=jnp.int32)
    named = jnp.any(routes_all[:, None] == every[None, :, None, None], axis=2)

    slots = n_dev * CAP
    egate = jnp.swapaxes(expert_gate, 1, 2)
    eup = jnp.swapaxes(expert_up, 1, 2)
    edown = jnp.swapaxes(expert_down, 1, 2)

    cot_blocks = cot_all.reshape(n_dev, tok, width)
    cot_rows = ein_b("bxst,btd->xbsd", pick_b, cot_blocks).reshape(n_local, slots, width)
    act_base = ein("xmd,xfd->xmf", cot_rows, edown)
    s_act_grad = ein("md,fd->mf", cot_all, sdown)

    normed_blocks = normed_all.reshape(n_dev, tok, width)
    logits = ein("btd,xd->bxt", normed_blocks, router_t)
    exps = jnp.where(named, jnp.exp(logits), 0.0)
    weights = exps / jnp.sum(exps, axis=1, keepdims=True)
    own_w = lax.dynamic_slice_in_dim(weights, e_rank * n_local, n_local, axis=1)
    slot_w = jnp.sum(jnp.where(pick, own_w[:, :, None, :], 0.0), axis=3)
    slot_w = slot_w.transpose(1, 0, 2).reshape(n_local, slots, 1)

    rows = ein_b("bxst,btd->xbsd", pick_b, normed_blocks).reshape(n_local, slots, width)
    gate = ein("xmd,xfd->xmf", rows, egate)
    upper = ein("xmd,xfd->xmf", rows, eup)
    sig = jax.nn.sigmoid(gate)
    active_f = gate * sig * upper
    active_w = (active_f * slot_w).astype(BF)
    dots = jnp.sum(active_f * act_base, axis=2)
    act_grad = act_base * slot_w
    up_part = (act_grad * gate * sig).astype(BF)
    gate_part = (act_grad * upper * sig * (1.0 + gate * (1.0 - sig))).astype(BF)

    s_gate = ein("md,fd->mf", normed_all, sgate)
    s_upper = ein("md,fd->mf", normed_all, sup)
    s_sig = jax.nn.sigmoid(s_gate)
    s_active = (s_gate * s_sig * s_upper).astype(BF)
    s_up_part = (s_act_grad * s_gate * s_sig).astype(BF)
    s_gate_part = (s_act_grad * s_upper * s_sig * (1.0 + s_gate * (1.0 - s_sig))).astype(BF)

    def combine(row_terms, token_terms):
        chunk = width // chunks
        done = []
        for c in range(chunks):
            cut = slice(c * chunk, (c + 1) * chunk)
            part = sum(ein("xmf,xfd->xmd", a, b[:, :, cut]) for a, b in row_terms).astype(BF)
            whole = ein("bxst,xbsd->btd", pick_b, part.reshape(n_local, n_dev, CAP, chunk))
            whole = whole.reshape(n_dev * tok, chunk)
            whole = whole + sum(ein("mf,fd->md", a, b[:, cut]) for a, b in token_terms)
            done.append(lax.psum_scatter(whole.astype(BF), ALL, scatter_dimension=0, tiled=True))
        return jnp.concatenate(done, axis=1).astype(F32)

    back_own = combine(
        [(gate_part, egate), (up_part, eup)], [(s_gate_part, sgate), (s_up_part, sup)]
    )
    out_own = combine([(active_w, edown)], [(s_active, sdown)])
    result = (middle + out_own).astype(BF)

    dots = dots.reshape(n_local, n_dev, CAP).transpose(1, 0, 2).reshape(n_dev, n_local * CAP)
    dots = lax.all_to_all(dots, ALL, split_axis=0, concat_axis=0, tiled=True)
    dots = jnp.sum(dots.reshape(n_ex, n_ws, n_local * CAP), axis=1).reshape(experts, CAP)
    _, mine = picks(routes.T[None], every)
    token_dots = jnp.sum(jnp.where(mine[0], dots[:, :, None], 0.0), axis=1)
    mine_w = lax.dynamic_index_in_dim(weights, d_rank, axis=0, keepdims=False)
    logit_grad = (
        mine_w * (token_dots - jnp.sum(mine_w * token_dots, axis=0, keepdims=True))
    ).astype(BF)
    router_grad = ein("xt,td->xd", logit_grad, normed)

    gate_grad = jnp.swapaxes(ein("xmf,xmd->xfd", gate_part, rows), 1, 2)
    up_grad = jnp.swapaxes(ein("xmf,xmd->xfd", up_part, rows), 1, 2)
    down_grad = jnp.swapaxes(ein("xmf,xmd->xfd", active_w, cot_rows), 1, 2)
    s_grads = jnp.stack(
        [
            ein("mf,md->fd", s_gate_part, normed_all),
            ein("mf,md->fd", s_up_part, normed_all),
            ein("mf,md->fd", s_active, cot_all),
        ],
        axis=0,
    ).astype(BF)
    s_grads = s_grads.reshape(3, fs_part, n_ws, d_part).transpose(2, 0, 1, 3)
    s_grads = lax.all_to_all(s_grads, WS, split_axis=0, concat_axis=0, tiled=True)
    s_grads = s_grads.transpose(1, 0, 2, 3).reshape(3, n_ws * fs_part, d_part)
    s_grads = jnp.swapaxes(s_grads, 1, 2).astype(F32)

    normed_grad = back_own + ein("xt,xd->td", logit_grad, router_t)
    middle_part, gain_two_grad = rms_back(middle, inverse_two, gain_two, normed_grad)
    middle_grad = cotangent.astype(F32) + middle_part

    m_g = gather_rel(middle_grad.astype(BF), WS).reshape(grp, width)
    out_w_grad = ein("mf,md->fd", context_flat, m_g)
    context_grad = (
        ein("md,fd->mf", m_g, w_out).astype(BF).reshape(n_ws, tok, heads, VH)
    )
    attn_back = jnp.where(
        allowed[:, None], jnp.exp(scores - jnp.log(totals)[..., None]), 0.0
    )
    value_grad = ein("bhij,bihd->bjhd", attn_back.astype(BF), context_grad)
    prob_grad = ein("bihd,bjhd->bhij", context_grad, values)
    delta = jnp.sum(context_grad.astype(F32) * context.astype(F32), axis=3).transpose(0, 2, 1)
    score_grad = (attn_back * (prob_grad - delta[..., None]) * scale_qk).astype(BF)
    query_grad = ein("bhij,bjhd->bihd", score_grad, key_vals)
    key_grad = ein("bhij,bihd->bjhd", score_grad, queries)
    query_back = rope_back(query_grad[..., NOPE:], cosine[:, :, None, :], sine[:, :, None, :])
    query_flat = (
        jnp.concatenate([query_grad[..., :NOPE], query_back], axis=3)
        .astype(BF)
        .reshape(grp, heads * hq)
    )
    kv_grad = (
        jnp.concatenate([key_grad[..., :NOPE], value_grad], axis=3)
        .astype(BF)
        .reshape(grp, heads * (NOPE + VH))
    )
    rope_sum = jnp.sum(key_grad[..., NOPE:], axis=2).reshape(grp, ROPE)
    latent_up = ein("mf,df->md", kv_grad, wkv)
    low = scatter_rel(
        jnp.concatenate([latent_up, rope_sum], axis=1).reshape(n_ws, tok, kvr + ROPE), WS
    )
    latent_grad, kv_gain_grad = rms_back(latent[:tok], inverse_kv[:tok], gain_kv, low[:, :kvr])
    rope_own = rope_back(low[:, kvr:], cosine[0], sine[0])
    low_grad = jnp.concatenate([latent_grad, rope_own], axis=1).astype(BF)
    hidden_up = scatter_rel(
        ein("mf,df->md", query_flat, wq).reshape(n_ws, tok, width), WS
    ) + ein("mf,df->md", low_grad, wdn)
    hidden_part, gain_one_grad = rms_back(inputs, inverse_g[:tok], gain_one, hidden_up)
    input_grad = (middle_grad + hidden_part).astype(BF)

    low_g = gather_rel(low_grad, WS).reshape(grp, kvr + ROPE)
    normed_cut = lax.dynamic_slice_in_dim(normed_in, w_rank * d_part, d_part, axis=1)
    kv_down_grad = ein("mf,md->fd", low_g, normed_cut)
    query_w_grad = ein("md,mf->df", normed_in, query_flat).astype(BF)
    kv_up_grad = ein("md,mf->df", latent_b, kv_grad).astype(BF)

    query_w_grad = query_w_grad.reshape(n_ws, d_part, heads * hq)
    kv_up_grad = kv_up_grad.reshape(n_ws, kv_part, heads * (NOPE + VH))

    def spread(grad):
        part = lax.psum_scatter(grad, EX, scatter_dimension=1, tiled=True)
        part = lax.all_to_all(part, WS, split_axis=0, concat_axis=2, tiled=True)
        return lax.all_gather(part[0], EX, axis=0, tiled=True).astype(F32)

    query_w_grad = spread(query_w_grad)
    kv_up_grad = spread(kv_up_grad)
    out_w_grad = lax.psum(out_w_grad.astype(BF), EX).astype(F32)
    kv_down_grad = lax.psum(kv_down_grad.astype(BF), EX).astype(F32).T

    small_grad = jnp.concatenate(
        [
            router_grad.reshape(experts, n_ws, d_part)
            .transpose(1, 0, 2)
            .reshape(n_ws, -1, lanes),
            gain_one_grad.reshape(n_ws, -1, lanes),
            gain_two_grad.reshape(n_ws, -1, lanes),
            kv_gain_grad.reshape(n_ws, -1, lanes),
        ],
        axis=1,
    )
    small_grad = lax.psum(small_grad, ALL)
    small_grad = lax.dynamic_index_in_dim(small_grad, w_rank, axis=0, keepdims=False)
    router_w_grad = small_grad[:r0].reshape(experts, d_part).T

    return (
        result,
        input_grad,
        small_grad[r0:r1].reshape(d_part),
        query_w_grad,
        kv_down_grad,
        small_grad[r2:r3].reshape(kv_part),
        kv_up_grad,
        out_w_grad,
        small_grad[r1:r2].reshape(d_part),
        router_w_grad,
        s_grads[0],
        s_grads[1],
        s_grads[2],
        gate_grad,
        up_grad,
        down_grad,
    )


def solution(mesh):
    both = P(ALL, None)
    in_specs = (
        both,
        both,
        both,
        P(WS),
        P(WS, None),
        P(WS, None),
        P(WS),
        P(WS, None),
        P(WS, None),
        P(WS),
        P(WS, None),
        P(WS, EX),
        P(WS, EX),
        P(WS, EX),
        P(EX, None, WS),
        P(EX, None, WS),
        P(EX, None, WS),
        both,
    )
    out_specs = (
        both,
        both,
        P(WS),
        P(WS, None),
        P(WS, None),
        P(WS),
        P(WS, None),
        P(WS, None),
        P(WS),
        P(WS, None),
        P(WS, EX),
        P(WS, EX),
        P(WS, EX),
        P(EX, None, WS),
        P(EX, None, WS),
        P(EX, None, WS),
    )
    return jax.shard_map(local, mesh=mesh, in_specs=in_specs, out_specs=out_specs, check_vma=False)
```

```python
import math

import jax
import jax.numpy as jnp
from jax import lax
from jax.experimental import pallas as pl
from jax.experimental.pallas import tpu as pltpu
from jax.experimental.layout import Layout, with_layout_constraint
from jax.sharding import PartitionSpec as P

NOPE = 128
ROPE = 64
VH = 128
CAP = 32
EPS = 1e-06
THETA = 50000.0

EX = "expert"
WS = "wshard"
ALL = (EX, WS)

BF = jnp.bfloat16
F32 = jnp.float32


def ein(form, left, right):
    return jnp.einsum(form, left, right, preferred_element_type=F32)


def ein_b(form, left, right):
    return jnp.einsum(form, left, right, preferred_element_type=BF)


def rms_norm(values, gain):
    inverse = lax.rsqrt(jnp.mean(values * values, axis=-1, keepdims=True) + EPS)
    return (values * inverse * gain, inverse)


def rms_back(values, inverse, gain, grad_in):
    scaled = grad_in * gain
    gain_grad = jnp.sum(grad_in * values * inverse, axis=0)
    moment = jnp.mean(scaled * values, axis=-1, keepdims=True)
    return (inverse * scaled - values * inverse**3 * moment, gain_grad)


def rope_tables(segment):
    places = jnp.arange(segment.shape[1], dtype=jnp.int32)
    earlier = jnp.sum((segment[:, None, :] < segment[:, :, None]).astype(jnp.int32), axis=2)
    position = (places[None, :] - earlier).astype(F32)
    inverse_freq = THETA ** (-jnp.arange(ROPE // 2, dtype=F32) * 2.0 / ROPE)
    angles = position[:, :, None] * inverse_freq[None, None, :]
    cosine = jnp.cos(angles)
    sine = jnp.sin(angles)
    return (
        jnp.concatenate([cosine, cosine], axis=2),
        jnp.concatenate([sine, sine], axis=2),
    )


def rotate_half(vector):
    half_size = vector.shape[-1] // 2
    return jnp.concatenate([-vector[..., half_size:], vector[..., :half_size]], axis=-1)


def apply_rope(vector, cosine, sine):
    return vector * cosine + rotate_half(vector) * sine


def rope_back(grad_in, cosine, sine):
    return grad_in * cosine - rotate_half(grad_in * sine)


def bits_of(size):
    bit = size // 2
    bits = []
    while bit:
        bits.append(bit)
        bit //= 2
    return bits


def swap(x, axis, bit):
    size = lax.axis_size(axis)
    return lax.ppermute(x, axis, [(i, i ^ bit) for i in range(size)])


def rel_ids(size):
    ids = [0]
    for bit in bits_of(size):
        ids = ids + [i ^ bit for i in ids]
    return ids


def gather_rel(x, axis):
    buf = x[None]
    for bit in bits_of(lax.axis_size(axis)):
        buf = jnp.concatenate([buf, swap(buf, axis, bit)], axis=0)
    return buf


def scatter_rel(x, axis):
    buf = x.astype(F32)
    for bit in reversed(bits_of(lax.axis_size(axis))):
        half = buf.shape[0] // 2
        other = swap(buf[half:].astype(BF), axis, bit)
        buf = buf[:half] + other.astype(F32)
    return buf[0]


def in_order(buf, axis):
    size = lax.axis_size(axis)
    ids = rel_ids(size)
    place = jnp.array([ids.index(i) for i in range(size)], dtype=jnp.int32)
    wanted = place[jnp.arange(size, dtype=jnp.int32) ^ lax.axis_index(axis)]
    return jnp.take(buf, wanted, axis=0)


def sum_all(x, axis):
    for bit in bits_of(lax.axis_size(axis)):
        x = x + swap(x, axis, bit)
    return x


def bit_order(axis):
    bits = bits_of(lax.axis_size(axis))
    return bits[-1:] + bits[:-1]


def halve(x, axis):
    rank = lax.axis_index(axis)
    for bit in bit_order(axis):
        half = x.shape[0] // 2
        high = ((rank & bit) != 0).astype(jnp.int32)
        keep = lax.dynamic_slice_in_dim(x, high * half, half, axis=0)
        send = lax.dynamic_slice_in_dim(x, (1 - high) * half, half, axis=0)
        x = (keep.astype(F32) + swap(send, axis, bit).astype(F32)).astype(BF)
    return x


def double(x, axis):
    rank = lax.axis_index(axis)
    for bit in reversed(bit_order(axis)):
        other = swap(x, axis, bit)
        x = jnp.where(
            (rank & bit) != 0,
            jnp.concatenate([other, x], axis=0),
            jnp.concatenate([x, other], axis=0),
        )
    return x


def split_step(x, left, step):
    axis, bit = step
    at = left.index(step)
    before, after = 2**at, 2 ** (len(left) - at - 1)
    x = x.reshape((before, 2, after) + x.shape[1:])
    high = ((lax.axis_index(axis) & bit) != 0).astype(jnp.int32)
    keep = lax.dynamic_index_in_dim(x, high, axis=1, keepdims=False)
    send = lax.dynamic_index_in_dim(x, 1 - high, axis=1, keepdims=False)
    left.pop(at)
    flat = (before * after,) + x.shape[3:]
    return keep.reshape(flat), swap(send, axis, bit).reshape(flat)


def join_halves(keep, other):
    return (keep.astype(F32) + other.astype(F32)).astype(BF)


def all_steps():
    return [(EX, bit) for bit in bits_of(lax.axis_size(EX))] + [
        (WS, bit) for bit in bits_of(lax.axis_size(WS))
    ]


def link_orders():
    ws_bits = [(WS, bit) for bit in reversed(bits_of(lax.axis_size(WS)))]
    ex_bits = [(EX, bit) for bit in bits_of(lax.axis_size(EX))]
    first, rest = ws_bits[:1], ws_bits[1:]
    return (first + rest + ex_bits[-1:] + ex_bits[:-1], first + ex_bits[-1:] + rest + ex_bits[:-1])


def dot_cols(left, right):
    return lax.dot_general(left, right, (((1,), (1,)), ((), ())), preferred_element_type=F32)


def dot_last(left, right):
    return jnp.dot(left, right, preferred_element_type=F32)


def act_parts(gate, upper, act_grad):
    sig = jax.nn.sigmoid(gate)
    active = gate * sig * upper
    up_part = act_grad * gate * sig
    gate_part = act_grad * upper * sig * (1.0 + gate * (1.0 - sig))
    return active, up_part, gate_part


def rows_kernel(
    normed, pick, pick_t, base, slot_w, gate_w, up_w, s_base, s_w,
    back, active_o, up_o, gate_o, dots_o, s_active_o, s_part_o,
    rows,
):
    blocks, tok, width = normed.shape
    n_local, group, _ = base.shape
    picked = pick.shape[1]
    cap = picked // n_local
    hidden_s = s_base.shape[1]

    def gather(d, carry):
        got = dot_last(pick[d], normed[d]).astype(BF)
        rows[d] = got.reshape(n_local, cap, width)
        return carry

    lax.fori_loop(0, blocks, gather, 0)

    def expert(j, carry):
        own = rows[:, j].reshape(group, width)
        gate_wj, up_wj = gate_w[j], up_w[j]
        gate = dot_cols(own, gate_wj)
        upper = dot_cols(own, up_wj)
        base_j, share = base[j], slot_w[j]
        active, up_part, gate_part = act_parts(gate, upper, base_j * share)
        active_o[j] = (active * share).astype(BF)
        dots_o[j] = jnp.sum(active * base_j, axis=1, keepdims=True)
        up_part, gate_part = up_part.astype(BF), gate_part.astype(BF)
        up_o[j] = up_part
        gate_o[j] = gate_part
        grad = dot_last(gate_part, gate_wj) + dot_last(up_part, up_wj)
        rows[:, j] = grad.astype(BF).reshape(blocks, cap, width)
        return carry

    lax.fori_loop(0, n_local, expert, 0)

    def finish(d, carry):
        both = dot_cols(normed[d], s_w[...])
        at = pl.multiple_of(d * tok, tok)
        active, up_part, gate_part = act_parts(
            both[:, :hidden_s], both[:, hidden_s:], s_base[pl.ds(at, tok), :]
        )
        s_active_o[pl.ds(at, tok), :] = active.astype(BF)
        part = jnp.concatenate([gate_part, up_part], axis=1).astype(BF)
        s_part_o[pl.ds(at, tok), :] = part
        grad = dot_last(pick_t[d], rows[d].reshape(picked, width)) + dot_last(part, s_w[...])
        back[d] = grad.astype(BF)
        return carry

    lax.fori_loop(0, blocks, finish, 0)


def rows_call(normed, pick, base, slot_w, gate_w, up_w, s_base, s_w):
    n_dev, tok, width = normed.shape
    n_local, slots, hidden_r = base.shape
    picked = pick.shape[1]
    hidden_s = s_base.shape[1]
    blocks = math.gcd(8, n_dev)
    group = slots * blocks // n_dev
    once = pl.Buffered(1)

    def whole(shape):
        return pl.BlockSpec(shape, lambda i: (0,) * len(shape), pipeline_mode=once)

    def lead(shape):
        return pl.BlockSpec(shape, lambda i: (i,) + (0,) * (len(shape) - 1))

    def middle(shape):
        return pl.BlockSpec(shape, lambda i: (0, i, 0))

    def out(*shape):
        return jax.ShapeDtypeStruct(shape, BF)

    part = middle((n_local, group, hidden_r))
    return pl.pallas_call(
        rows_kernel,
        grid=(n_dev // blocks,),
        in_specs=[
            lead((blocks, tok, width)),
            lead((blocks, picked, tok)),
            lead((blocks, tok, picked)),
            part,
            middle((n_local, group, 1)),
            whole(gate_w.shape),
            whole(up_w.shape),
            lead((blocks * tok, hidden_s)),
            whole(s_w.shape),
        ],
        out_specs=[
            lead((blocks, tok, width)),
            part,
            part,
            part,
            middle((n_local, group, 1)),
            lead((blocks * tok, hidden_s)),
            lead((blocks * tok, 2 * hidden_s)),
        ],
        out_shape=[
            out(n_dev, tok, width),
            out(n_local, slots, hidden_r),
            out(n_local, slots, hidden_r),
            out(n_local, slots, hidden_r),
            jax.ShapeDtypeStruct((n_local, slots, 1), F32),
            out(n_dev * tok, hidden_s),
            out(n_dev * tok, 2 * hidden_s),
        ],
        scratch_shapes=[pltpu.VMEM((blocks, n_local, picked // n_local, width), BF)],
        compiler_params=pltpu.CompilerParams(
            dimension_semantics=("arbitrary",), vmem_limit_bytes=60 * 2**20
        ),
        name="rows_step",
    )(normed, pick, jnp.swapaxes(pick, 1, 2), base, slot_w, gate_w, up_w, s_base, s_w)


def local(
    hidden,
    segment_ids,
    routes,
    attn_gain,
    w_query,
    w_kv_down,
    kv_gain,
    w_kv_up,
    w_out,
    ffn_gain,
    w_router,
    shared_gate,
    shared_up,
    shared_down,
    expert_gate,
    expert_up,
    expert_down,
    cotangent,
):
    n_ex = lax.axis_size(EX)
    n_ws = lax.axis_size(WS)
    n_dev = n_ex * n_ws
    e_rank = lax.axis_index(EX)
    w_rank = lax.axis_index(WS)
    d_rank = e_rank * n_ws + w_rank
    tok, width = hidden.shape
    top = routes.shape[1]
    d_part = w_query.shape[0]
    kv_part = w_kv_up.shape[0]
    kvr = kv_part * n_ws
    heads = w_out.shape[0] // VH
    hq = NOPE + ROPE
    n_local = expert_gate.shape[0]
    experts = n_local * n_ex
    fs_part = shared_gate.shape[1] // n_ws
    lanes = 128
    chunks = max(1, n_dev // 32)

    small = jnp.concatenate(
        [
            w_router.T.reshape(-1, lanes),
            attn_gain.reshape(-1, lanes),
            ffn_gain.reshape(-1, lanes),
            kv_gain.reshape(-1, lanes),
            segment_ids.astype(BF).reshape(-1, lanes),
        ],
        axis=0,
    )
    small = in_order(gather_rel(small, WS), WS)
    r0 = experts * d_part // lanes
    r1 = r0 + d_part // lanes
    r2 = r1 + d_part // lanes
    r3 = r2 + kv_part // lanes
    router_t = (
        small[:, :r0].reshape(n_ws, experts, d_part).transpose(1, 0, 2).reshape(experts, width)
    )
    gain_one = small[:, r0:r1].reshape(width).astype(F32)
    gain_two = small[:, r1:r2].reshape(width).astype(F32)
    gain_kv = small[:, r2:r3].reshape(kvr).astype(F32)
    segment_abs = small[:, r3:].reshape(n_ws, tok).astype(jnp.int32)
    ids = jnp.array(rel_ids(n_ws), dtype=jnp.int32)
    segment = jnp.take(segment_abs, w_rank ^ ids, axis=0)

    hidden_g = gather_rel(hidden, WS)
    rows_first = Layout(major_to_minor=(0, 1, 2))

    def to_heads(weight):
        parts = weight.reshape(weight.shape[0], n_ws, -1).transpose(1, 0, 2)
        parts = with_layout_constraint(parts, rows_first)
        parts = lax.all_to_all(parts, WS, split_axis=0, concat_axis=0, tiled=True)
        parts = with_layout_constraint(parts, rows_first)
        return parts.reshape(-1, parts.shape[2])

    def to_heads_p(weight):
        parts = weight.reshape(weight.shape[0], n_ws, -1)
        got = []
        for r in rel_ids(n_ws):
            part = lax.dynamic_index_in_dim(parts, w_rank ^ r, axis=1, keepdims=False)
            if r:
                part = lax.ppermute(part, WS, [(i, i ^ r) for i in range(n_ws)])
            got.append(part)
        got = in_order(jnp.stack(got, axis=0), WS)
        return got.reshape(-1, got.shape[2])

    wq = to_heads(w_query)
    wkv = to_heads_p(w_kv_up)
    wdn = in_order(gather_rel(w_kv_down.T, WS), WS)

    grp = n_ws * tok
    cosine, sine = rope_tables(segment)
    scale_qk = 1.0 / math.sqrt(hq)
    inputs_g = hidden_g.reshape(grp, width).astype(F32)
    normed_f, inverse_g = rms_norm(inputs_g, gain_one)
    normed_in = normed_f.astype(BF)
    query_f = ein("md,df->mf", normed_in, wq).reshape(n_ws, tok, heads, hq)
    query_rot = apply_rope(query_f[..., NOPE:], cosine[:, :, None, :], sine[:, :, None, :])
    queries = jnp.concatenate([query_f[..., :NOPE], query_rot], axis=3).astype(BF)
    wdn = wdn.transpose(1, 0, 2).reshape(kvr + ROPE, width)
    lowered = ein("md,fd->mf", normed_in, wdn)
    latent = lowered[:, :kvr]
    latent_f, inverse_kv = rms_norm(latent, gain_kv)
    latent_b = latent_f.astype(BF)
    key_rope = apply_rope(lowered[:, kvr:].reshape(n_ws, tok, ROPE), cosine, sine)
    raised_kv = ein("md,df->mf", latent_b, wkv).reshape(n_ws, tok, heads, NOPE + VH)
    key_vals = jnp.concatenate(
        [
            raised_kv[..., :NOPE],
            jnp.broadcast_to(key_rope[:, :, None, :], (n_ws, tok, heads, ROPE)),
        ],
        axis=3,
    ).astype(BF)
    values = raised_kv[..., NOPE:].astype(BF)
    places = jnp.arange(tok, dtype=jnp.int32)
    allowed = (segment[:, :, None] == segment[:, None, :]) & (
        places[None, None, :] <= places[None, :, None]
    )
    scores = ein("bihd,bjhd->bhij", queries, key_vals) * scale_qk
    raised = jnp.where(allowed[:, None], jnp.exp(scores), 0.0)
    totals = jnp.sum(raised, axis=3)
    attn_probs = (raised / totals[..., None]).astype(BF)
    context = ein("bhij,bjhd->bihd", attn_probs, values).astype(BF)
    context_flat = context.reshape(grp, heads * VH)
    mixed = scatter_rel(ein("mf,fd->md", context_flat, w_out).reshape(n_ws, tok, width), WS)
    inputs = hidden.astype(F32)
    middle = inputs + mixed
    normed_two, inverse_two = rms_norm(middle, gain_two)
    normed = normed_two.astype(BF)

    cot_all = lax.all_gather(cotangent, ALL, axis=0, tiled=True)
    routes_all = in_order(gather_rel(in_order(gather_rel(routes.T, WS), WS), EX), EX)
    routes_all = routes_all.reshape(n_dev, top, tok)
    normed_all = lax.all_gather(normed, ALL, axis=0, tiled=True)

    shared = jnp.stack([shared_gate.T, shared_up.T, shared_down.T], axis=0)
    shared = shared.reshape(3, n_ws, fs_part, d_part).transpose(1, 0, 2, 3)
    shared = lax.all_to_all(shared, WS, split_axis=0, concat_axis=0, tiled=True)
    shared = shared.transpose(1, 2, 0, 3).reshape(3, fs_part, width)
    sgate, sup, sdown = shared[0], shared[1], shared[2]

    tri = (places[:, None] < places[None, :]).astype(BF)

    def picks(table, wanted):
        hit = jnp.any(table[:, None] == wanted[None, :, None, None], axis=2)
        rank = ein("bxs,st->bxt", hit.astype(BF), tri).astype(jnp.int32)
        slot = jnp.arange(CAP, dtype=jnp.int32)
        return hit, (hit[:, :, None, :] & (rank[:, :, None, :] == slot[None, None, :, None]))

    own_experts = e_rank * n_local + jnp.arange(n_local, dtype=jnp.int32)
    _, pick = picks(routes_all, own_experts)
    pick_b = pick.astype(BF)
    every = jnp.arange(experts, dtype=jnp.int32)
    named = jnp.any(routes.T[None] == every[:, None, None], axis=1)
    exps = jnp.where(named, jnp.exp(ein("xd,td->xt", router_t, normed)), 0.0)
    mine_w = exps / jnp.sum(exps, axis=0, keepdims=True)
    weights = in_order(gather_rel(in_order(gather_rel(mine_w, WS), WS), EX), EX)
    weights = weights.reshape(n_dev, experts, tok)

    slots = n_dev * CAP
    egate = jnp.swapaxes(expert_gate, 1, 2)
    eup = jnp.swapaxes(expert_up, 1, 2)
    edown = jnp.swapaxes(expert_down, 1, 2)

    cot_blocks = cot_all.reshape(n_dev, tok, width)
    cot_rows = ein_b("bxst,btd->xbsd", pick_b, cot_blocks).reshape(n_local, slots, width)
    act_base = ein("xmd,xfd->xmf", cot_rows, edown)
    s_fill = ((0, -fs_part % lanes), (0, 0))
    sgate, sup, sdown = (jnp.pad(part, s_fill) for part in (sgate, sup, sdown))
    fs_pad = sdown.shape[0]
    s_act_grad = ein("md,fd->mf", cot_all, sdown)

    normed_blocks = normed_all.reshape(n_dev, tok, width)
    own_w = lax.dynamic_slice_in_dim(weights, e_rank * n_local, n_local, axis=1)
    slot_w = jnp.sum(jnp.where(pick, own_w[:, :, None, :], 0.0), axis=3)
    slot_w = slot_w.transpose(1, 0, 2).reshape(n_local, slots, 1)

    back_all, active_w, up_part, gate_part, dots, s_active, s_part = rows_call(
        normed_blocks,
        pick_b.reshape(n_dev, n_local * CAP, tok),
        act_base,
        slot_w,
        egate,
        eup,
        s_act_grad,
        jnp.concatenate([sgate, sup], axis=0),
    )
    rows = ein_b("bxst,btd->xbsd", pick_b, normed_blocks).reshape(n_local, slots, width)

    chunk = width // chunks

    def combine(cut, part, weight, token_part, token_weight):
        rows_out = ein_b("xmf,xfd->xmd", part, weight[:, :, cut])
        whole = ein("bxst,xbsd->btd", pick_b, rows_out.reshape(n_local, n_dev, CAP, chunk))
        return (
            whole.reshape(n_dev * tok, chunk) + ein("mf,fd->md", token_part, token_weight[:, cut])
        ).astype(BF)

    cuts = [slice(c * chunk, (c + 1) * chunk) for c in range(chunks)]
    back_own = lax.psum_scatter(
        back_all.reshape(n_dev * tok, width), ALL, scatter_dimension=0, tiled=True
    ).astype(F32)
    started = []
    for cut in cuts:
        out_all = combine(cut, active_w, edown, s_active, sdown).reshape(n_dev, tok, chunk)
        mid = chunk // 2
        for order, half in zip(link_orders(), (out_all[:, :, :mid], out_all[:, :, mid:])):
            left = all_steps()
            half = join_halves(*split_step(half, left, order[0]))
            started.append((*split_step(half, left, order[1]), left, order[2:]))

    dots = dots.reshape(n_local, n_dev, CAP).transpose(1, 0, 2).reshape(n_dev, n_local * CAP)
    dots = lax.all_to_all(dots, ALL, split_axis=0, concat_axis=0, tiled=True)
    dots = jnp.sum(dots.reshape(n_ex, n_ws, n_local * CAP), axis=1).reshape(experts, CAP)
    _, mine = picks(routes.T[None], every)
    token_dots = jnp.sum(jnp.where(mine[0], dots[:, :, None], 0.0), axis=1)
    logit_grad = (
        mine_w * (token_dots - jnp.sum(mine_w * token_dots, axis=0, keepdims=True))
    ).astype(BF)
    router_grad = ein("xt,td->xd", logit_grad, normed)

    gate_grad = jnp.swapaxes(ein("xmf,xmd->xfd", gate_part, rows), 1, 2)
    up_grad = jnp.swapaxes(ein("xmf,xmd->xfd", up_part, rows), 1, 2)
    down_grad = jnp.swapaxes(ein("xmf,xmd->xfd", active_w, cot_rows), 1, 2)
    s_both = ein("mf,md->fd", s_part, normed_all).astype(BF)
    s_down = ein("mf,md->fd", s_active, cot_all).astype(BF)
    s_grads = jnp.stack(
        [s_both[:fs_part], s_both[fs_pad : fs_pad + fs_part], s_down[:fs_part]], axis=0
    )
    s_grads = s_grads.reshape(3, fs_part, n_ws, d_part).transpose(2, 0, 1, 3)
    s_grads = lax.all_to_all(s_grads, WS, split_axis=0, concat_axis=0, tiled=True)
    s_grads = s_grads.transpose(1, 0, 2, 3).reshape(3, n_ws * fs_part, d_part)
    s_grads = jnp.swapaxes(s_grads, 1, 2).astype(F32)

    normed_grad = back_own + ein("xt,xd->td", logit_grad, router_t)
    middle_part, gain_two_grad = rms_back(middle, inverse_two, gain_two, normed_grad)
    middle_grad = cotangent.astype(F32) + middle_part

    m_g = gather_rel(middle_grad.astype(BF), WS).reshape(grp, width)
    out_w_grad = ein("mf,md->fd", context_flat, m_g)
    out_w_grad = halve(out_w_grad.astype(BF), EX)
    context_grad = (
        ein("md,fd->mf", m_g, w_out).astype(BF).reshape(n_ws, tok, heads, VH)
    )
    attn_back = jnp.where(
        allowed[:, None], jnp.exp(scores - jnp.log(totals)[..., None]), 0.0
    )
    value_grad = ein("bhij,bihd->bjhd", attn_back.astype(BF), context_grad)
    prob_grad = ein("bihd,bjhd->bhij", context_grad, values)
    delta = jnp.sum(context_grad.astype(F32) * context.astype(F32), axis=3).transpose(0, 2, 1)
    score_grad = (attn_back * (prob_grad - delta[..., None]) * scale_qk).astype(BF)
    query_grad = ein("bhij,bjhd->bihd", score_grad, key_vals)
    key_grad = ein("bhij,bihd->bjhd", score_grad, queries)
    query_back = rope_back(query_grad[..., NOPE:], cosine[:, :, None, :], sine[:, :, None, :])
    query_flat = (
        jnp.concatenate([query_grad[..., :NOPE], query_back], axis=3)
        .astype(BF)
        .reshape(grp, heads * hq)
    )
    kv_grad = (
        jnp.concatenate([key_grad[..., :NOPE], value_grad], axis=3)
        .astype(BF)
        .reshape(grp, heads * (NOPE + VH))
    )
    query_flat, kv_grad, out_w_grad, held = lax.optimization_barrier(
        (query_flat, kv_grad, out_w_grad, [pair[:2] for pair in started])
    )
    rope_sum = jnp.sum(key_grad[..., NOPE:], axis=2).reshape(grp, ROPE)
    latent_up = ein("mf,df->md", kv_grad, wkv)
    low = scatter_rel(
        jnp.concatenate([latent_up, rope_sum], axis=1).reshape(n_ws, tok, kvr + ROPE), WS
    )
    latent_grad, kv_gain_grad = rms_back(latent[:tok], inverse_kv[:tok], gain_kv, low[:, :kvr])
    rope_own = rope_back(low[:, kvr:], cosine[0], sine[0])
    low_grad = jnp.concatenate([latent_grad, rope_own], axis=1).astype(BF)
    hidden_up = scatter_rel(
        ein("mf,df->md", query_flat, wq).reshape(n_ws, tok, width), WS
    ) + ein("mf,fd->md", low_grad, wdn)
    hidden_part, gain_one_grad = rms_back(inputs, inverse_g[:tok], gain_one, hidden_up)
    input_grad = (middle_grad + hidden_part).astype(BF)
    low_g = gather_rel(low_grad, WS).reshape(grp, kvr + ROPE)
    normed_cut = lax.dynamic_slice_in_dim(normed_in, w_rank * d_part, d_part, axis=1)
    kv_down_grad = ein("mf,md->fd", low_g, normed_cut)
    query_w_grad = ein("md,mf->df", normed_in, query_flat).astype(BF)
    kv_up_grad = ein("md,mf->df", latent_b, kv_grad).astype(BF)

    query_w_grad = query_w_grad.reshape(n_ws, d_part, heads * hq)
    kv_up_grad = kv_up_grad.reshape(n_ws, kv_part, heads * (NOPE + VH))

    part = lax.psum_scatter(query_w_grad, EX, scatter_dimension=1, tiled=True)
    part = lax.all_to_all(part, WS, split_axis=0, concat_axis=2, tiled=True)
    query_w_grad = lax.all_gather(part[0], EX, axis=0, tiled=True).astype(F32)
    part = halve(kv_up_grad.transpose(1, 0, 2), EX)
    part = lax.all_to_all(part, WS, split_axis=1, concat_axis=2, tiled=True)
    kv_up_grad = double(part[:, 0], EX).astype(F32)
    out_w_grad = double(out_w_grad, EX).astype(F32)

    small_grad = jnp.concatenate(
        [
            router_grad.reshape(experts, n_ws, d_part)
            .transpose(1, 0, 2)
            .reshape(n_ws, -1, lanes),
            gain_one_grad.reshape(n_ws, -1, lanes),
            gain_two_grad.reshape(n_ws, -1, lanes),
            kv_gain_grad.reshape(n_ws, -1, lanes),
        ],
        axis=1,
    )
    small_grad = jnp.take(small_grad, w_rank ^ ids, axis=0)
    for bit in reversed(bits_of(n_ws)):
        half = small_grad.shape[0] // 2
        small_grad = small_grad[:half] + swap(small_grad[half:], WS, bit)
    small_grad = small_grad[0].astype(BF).reshape(-1)
    low_rows = kvr + ROPE
    all_rows = low_rows + -(-small_grad.shape[0] // d_part)
    all_rows = all_rows + -all_rows % (16 * n_ex)
    small_size = small_grad.shape[0]
    small_grad = jnp.pad(small_grad, (0, (all_rows - low_rows) * d_part - small_size))
    late = jnp.concatenate([kv_down_grad.astype(BF), small_grad.reshape(-1, d_part)], axis=0)
    late = double(halve(late, EX), EX).astype(F32)
    kv_down_grad = late[:low_rows].T
    small_grad = late[low_rows:].reshape(-1)[:small_size].reshape(-1, lanes)
    router_w_grad = small_grad[:r0].reshape(experts, d_part).T

    out_halves = []
    for (keep, other), (_, _, left, order) in zip(held, started):
        for step in order:
            keep, other = split_step(join_halves(keep, other), left, step)
        out_halves.append(join_halves(keep, other)[0])
    out_own = jnp.concatenate(out_halves, axis=1).astype(F32)
    out_own, middle_late, input_grad = lax.optimization_barrier((out_own, middle, input_grad))
    result = (middle_late + out_own).astype(BF)

    return (
        result,
        input_grad,
        small_grad[r0:r1].reshape(d_part),
        query_w_grad,
        kv_down_grad,
        small_grad[r2:r3].reshape(kv_part),
        kv_up_grad,
        out_w_grad,
        small_grad[r1:r2].reshape(d_part),
        router_w_grad,
        s_grads[0],
        s_grads[1],
        s_grads[2],
        gate_grad,
        up_grad,
        down_grad,
    )


def solution(mesh):
    both = P(ALL, None)
    in_specs = (
        both,
        both,
        both,
        P(WS),
        P(WS, None),
        P(WS, None),
        P(WS),
        P(WS, None),
        P(WS, None),
        P(WS),
        P(WS, None),
        P(WS, EX),
        P(WS, EX),
        P(WS, EX),
        P(EX, None, WS),
        P(EX, None, WS),
        P(EX, None, WS),
        both,
    )
    out_specs = (
        both,
        both,
        P(WS),
        P(WS, None),
        P(WS, None),
        P(WS),
        P(WS, None),
        P(WS, None),
        P(WS),
        P(WS, None),
        P(WS, EX),
        P(WS, EX),
        P(WS, EX),
        P(EX, None, WS),
        P(EX, None, WS),
        P(EX, None, WS),
    )
    return jax.shard_map(local, mesh=mesh, in_specs=in_specs, out_specs=out_specs, check_vma=False)
```
